32 devices in a mesh: along: 2 (over core), across: 4 (over y, x), chan: 4 (over z).
Axes of the slice: x: 2, y: 2, z: 4, core: 2. Of those that a mesh axis runs over, the one named last changes fastest.
Arguments:
- jacobian: float32 [8, 32, 512, 384], P('along', 'across', 'chan'), may hold values from -0.3125 to 0.3125
- departures: float32 [8, 32, 512], P('along', 'across', 'chan'), may hold values from -6 to 6
- inv_variance: float32 [512], P('chan'), may hold values from 0.3 to 3
- channel_use: int32 [512], P('chan'), may hold values 0 or 1
- clear_flags: int32 [8, 32], P('along', 'across'), may hold values 0 or 1
- coefficients: float32 [25, 384], replicated, may hold values from -1.25 to 1.25
Outputs:
- control: float32 [8, 32, 384], P('along', 'across')
- increment: float32 [8, 32, 384], P('along', 'across')
- residual: float32 [8, 32, 384], P('along', 'across')
The draws below stay inside these ranges and needn't reach their ends.
All inputs are finite; a program needn't handle non-finite values. No bound on the sum of `channel_use` or of `clear_flags` on one device may be relied on, other than what follows from the above.
Results may differ from the reference program's by a relative error of at most 0.0003.
Values sent between devices are 32-bit elements; how exact they have to be, the bound alone decides.
A program may use at most 64 MiB of HBM per device.

```python
import math
import jax
import jax.numpy as jnp
from jax import lax

CH = 512
ITERS = 10
S = 384
NX = 8
NY = 32


def set_ends(drawn, rng, smallest, top_value):
    extent = drawn.shape
    place = [jax.random.randint(jax.random.fold_in(rng, axis), (), 0, extent[axis]) for axis in range(len(extent))]
    drawn = drawn.at[tuple(place)].set(smallest)
    longest = extent.index(max(extent))
    place[longest] = (place[longest] + 1) % extent[longest]
    return drawn.at[tuple(place)].set(top_value)


def block_levels(stream_key, shape, pieces, least, top_value):
    gain, own = 1.0, jax.random.fold_in(stream_key, 6)
    for dim, shards_of in pieces:
        steps = jnp.exp(jax.random.uniform(jax.random.fold_in(own, dim), (shards_of,), jnp.float32, least / len(pieces), top_value / len(pieces)))
        gain = gain * jnp.repeat(steps, shape[dim] // shards_of).reshape([-1 if axis == dim else 1 for axis in range(len(shape))])
    return gain


def noise(stream_key, extent, width, reach, shards=(), kind=jnp.bfloat16):
    values = jax.random.normal(stream_key, extent, jnp.float32) * width
    if len(shards) > 0:
        values = block_levels(stream_key, extent, shards, -0.22, 0.18) * values
    return jnp.clip(values, min=-reach, max=reach).astype(kind)


def setup_inputs(seed: int = 0) -> dict:
    key_of = jax.random.split(jax.random.key(seed), 7)
    jacobian = noise(key_of[0], (NX, NY, CH, S), S ** -0.5, 0.3125, ((0, 2), (1, 4), (2, 4)), jnp.float32)
    departures = noise(key_of[1], (NX, NY, CH), 1.0, 6.0, ((0, 2), (1, 4), (2, 4)), jnp.float32)
    inv_variance = jnp.clip(jnp.exp(math.log(3.0) - 2.3025851 * jax.random.uniform(key_of[2], (CH,), jnp.float32) ** block_levels(key_of[2], (CH,), ((0, 4),), -0.2, 0.2)), 0.3, 3.0)
    channel_use = set_ends((jax.random.randint(key_of[3], (CH,), 0, 4) < 3).astype(jnp.int32), jax.random.fold_in(key_of[3], 1), 0, 1)
    clear_flags = set_ends((jax.random.randint(key_of[4], (NX, NY), 0, 4) < 3).astype(jnp.int32), jax.random.fold_in(key_of[4], 1), 0, 1)
    coefficients = noise(key_of[5], (25, S), 25 ** -0.5, 1.25, (), jnp.float32)
    return {"jacobian": jacobian, "departures": departures, "inv_variance": inv_variance, "channel_use": channel_use, "clear_flags": clear_flags, "coefficients": coefficients}


def spread(field, coefficients):
    rows_here, cols_here = field.shape[0], field.shape[1]
    padded = jnp.pad(field, ((2, 2), (2, 2), (0, 0)))
    result = jnp.zeros(field.shape, jnp.float32)
    for row_shift in range(5):
        for col_shift in range(5):
            result = result + coefficients[row_shift * 5 + col_shift] * padded[row_shift:row_shift + rows_here, col_shift:col_shift + cols_here]
    return result


def spread_back(field, coefficients):
    rows_here, cols_here = field.shape[0], field.shape[1]
    padded = jnp.pad(field, ((2, 2), (2, 2), (0, 0)))
    result = jnp.zeros(field.shape, jnp.float32)
    for row_shift in range(5):
        for col_shift in range(5):
            result = result + coefficients[row_shift * 5 + col_shift] * padded[4 - row_shift:4 - row_shift + rows_here, 4 - col_shift:4 - col_shift + cols_here]
    return result


def reference(jacobian, departures, inv_variance, channel_use, clear_flags, coefficients):
    weight = inv_variance[None, None, :] * channel_use.astype(jnp.float32)[None, None, :] * clear_flags.astype(jnp.float32)[:, :, None]

    def forward(field):
        return jnp.einsum('xycs,xys->xyc', jacobian, field, precision=lax.Precision.HIGHEST)

    def adjoint(weighted):
        return jnp.einsum('xycs,xyc->xys', jacobian, weighted, precision=lax.Precision.HIGHEST)

    def hessian(direction):
        return direction + spread_back(adjoint(weight * forward(spread(direction, coefficients))), coefficients)

    rhs = spread_back(adjoint(weight * departures), coefficients)
    control = jnp.zeros_like(rhs)
    residual = rhs
    direction = rhs
    norm_now = jnp.sum(residual * residual)
    for step_index in range(ITERS):
        image = hessian(direction)
        alpha = norm_now / jnp.sum(direction * image)
        control = control + alpha * direction
        residual = residual - alpha * image
        fresh_norm = jnp.sum(residual * residual)
        direction = residual + (fresh_norm / norm_now) * direction
        norm_now = fresh_norm
    return control, spread(control, coefficients), residual
```

```python
import functools

import jax
import jax.numpy as jnp
from jax import lax
from jax.experimental import pallas as pl
from jax.experimental.pallas import tpu as pltpu
from jax.sharding import PartitionSpec as P

ITERS = 10
RIM = 2
WIDE = 2 * RIM
TAPS = 2 * RIM + 1
PACK = 4
MESH = pl.DeviceIdType.MESH


def kernel(
    dims, jac_hbm, dep_ref, var_ref, use_ref, flag_ref, coef_ref,
    ctl_ref, inc_ref, res_ref,
    jac, wt, coef, part, wide, sums, urs, fr, fd, fc, fx, keep,
    jac_sem, chan_send, chan_recv, rim_send, rim_recv, sum_send, sum_recv,
):
    n_along, n_across, n_chan = dims
    rows, cols, chans, _ = jac.shape
    lanes = part.shape[-1]
    tiles = coef_ref.shape[1] // lanes
    ext_r, ext_c = rows + 2 * RIM, cols + 2 * RIM
    group = n_along * n_across
    f32 = jnp.float32

    a_me = lax.axis_index("along")
    x_me = lax.axis_index("across")
    c_me = lax.axis_index("chan")
    g_me = a_me * n_across + x_me

    loads = [
        pltpu.make_async_copy(jac_hbm.at[i], jac.at[i], jac_sem.at[i]) for i in range(rows)
    ]
    for load in loads:
        load.start()

    wide[...] = jnp.zeros_like(wide)
    sums[...] = jnp.zeros_like(sums)
    urs[...] = jnp.zeros_like(urs)
    fd[...] = jnp.zeros_like(fd)
    fc[...] = jnp.zeros_like(fc)
    fx[...] = jnp.zeros_like(fx)
    coef[...] = jnp.zeros_like(coef)
    keep[...] = jnp.ones_like(keep)

    chan_peers = [lax.rem(c_me + d, n_chan) for d in range(1, n_chan)]
    group_peers = []
    for d in range(1, group):
        peer = lax.rem(g_me + d, group)
        group_peers.append((peer // n_across, lax.rem(peer, n_across)))

    barrier = pltpu.get_barrier_semaphore()
    for c in chan_peers:
        pl.semaphore_signal(barrier, inc=1, device_id={"chan": c}, device_id_type=MESH)
    for a, x in group_peers:
        pl.semaphore_signal(
            barrier, inc=1, device_id={"along": a, "across": x}, device_id_type=MESH
        )
    pl.semaphore_wait(barrier, len(chan_peers) + len(group_peers))

    for t in range(TAPS * TAPS):
        for l in range(tiles):
            row = coef_ref[t : t + 1, l * lanes : (l + 1) * lanes]
            coef[t, l : l + 1, :] = row
            coef[t, PACK + l : PACK + l + 1, :] = row

    chan_weight = var_ref[...] * use_ref[...].astype(f32)
    wd = dep_ref[...].reshape(rows * cols, chans) * chan_weight
    stack = jnp.concatenate([wd, jnp.broadcast_to(chan_weight, (8, chans))], axis=0)
    turned = jnp.transpose(stack)
    blocks = chans // 8
    for k in range(blocks):
        wt[k] = jnp.broadcast_to(
            turned[k * 8 : (k + 1) * 8, rows * cols : rows * cols + 1], (8, lanes)
        )

    def chan_copy(par, i, d):
        place = part.at[par, c_me, pl.ds(i * tiles * cols, tiles * cols)]
        return pltpu.make_async_remote_copy(
            src_ref=place, dst_ref=place,
            send_sem=chan_send.at[par, i, d], recv_sem=chan_recv.at[par, i, d],
            device_id={"chan": chan_peers[d]}, device_id_type=MESH,
        )

    def store_part(par, i, j, accs):
        for l in range(tiles):
            part[par, c_me, pl.ds((i * tiles + l) * cols + j, 1), :] = jnp.sum(
                accs[l], axis=0, keepdims=True
            )

    sides = []
    for da in (-1, 0, 1):
        for dx in (-1, 0, 1):
            if da == 0 and dx == 0:
                continue
            here = None
            for delta, me, count in ((da, a_me, n_along), (dx, x_me, n_across)):
                if delta:
                    ok = me > 0 if delta < 0 else me < count - 1
                    here = ok if here is None else jnp.logical_and(here, ok)
            if da and n_along == 1 or dx and n_across == 1:
                continue

            def span(delta, size):
                if delta == 0:
                    return WIDE, size, WIDE
                if delta < 0:
                    return WIDE, WIDE, WIDE + size
                return size, WIDE, 0

            sides.append((da, dx, here, span(da, rows), span(dx, cols)))

    def rim_copy(par, n):
        da, dx, _, (r0, rn, rt), (c0, cn, ct) = sides[n]
        return pltpu.make_async_remote_copy(
            src_ref=wide.at[par, pl.ds(r0, rn), pl.ds(c0 * PACK, cn * PACK)],
            dst_ref=wide.at[par, pl.ds(rt, rn), pl.ds(ct * PACK, cn * PACK)],
            send_sem=rim_send.at[par, n], recv_sem=rim_recv.at[par, n],
            device_id={"along": a_me + da, "across": x_me + dx}, device_id_type=MESH,
        )

    opposite = {
        n: next(m for m, t in enumerate(sides) if (t[0], t[1]) == (-s[0], -s[1]))
        for n, s in enumerate(sides)
    }

    def sum_copy(par, d):
        a, x = group_peers[d]
        place = sums.at[par, g_me]
        return pltpu.make_async_remote_copy(
            src_ref=place, dst_ref=place,
            send_sem=sum_send.at[par, d], recv_sem=sum_recv.at[par, d],
            device_id={"along": a, "across": x}, device_id_type=MESH,
        )

    def finish_chan(par):
        for i in range(rows):
            for d in range(n_chan - 1):
                chan_copy(par, i, d).wait_recv()
            for l in range(tiles):
                at = pl.ds((i * tiles + l) * cols, cols)
                total = part[par, 0, at, :]
                for c in range(1, n_chan):
                    total = total + part[par, c, at, :]
                wide[par, WIDE + i, pl.ds(WIDE * PACK + l, cols, stride=PACK), :] = total

    def start_rims(par):
        for n, side in enumerate(sides):
            @pl.when(side[2])
            def _():
                rim_copy(par, n).start()

    def finish_rims(par):
        for n, side in enumerate(sides):
            @pl.when(side[2])
            def _():
                rim_copy(par, opposite[n]).wait_recv()

    def finish_sends(par):
        for i in range(rows):
            for d in range(n_chan - 1):
                chan_copy(par, i, d).wait_send()
        for n, side in enumerate(sides):
            @pl.when(side[2])
            def _():
                rim_copy(par, n).wait_send()

    one, zero = jnp.float32(1), jnp.float32(0)
    row_edge = (
        jnp.where(a_me > 0, one, zero), jnp.where(a_me < n_along - 1, one, zero)
    )
    col_edge = (
        jnp.where(x_me > 0, one, zero), jnp.where(x_me < n_across - 1, one, zero)
    )
    pairs = ext_c // 2

    def spread_back_row(par, e):
        accs = [jnp.zeros((8, lanes), f32) for _ in range(pairs)]
        for a in range(TAPS):
            for b in range(TAPS):
                c = coef[a * TAPS + b]
                for g in range(pairs):
                    accs[g] = accs[g] + c * wide[
                        par, e + WIDE - a, pl.ds(8 * g + (WIDE - b) * PACK, 8), :
                    ]
        for g in range(pairs):
            scale = None
            if e < RIM or e >= RIM + rows:
                scale = row_edge[0 if e < RIM else 1]
            if g < RIM // 2 or g >= (RIM + cols) // 2:
                edge = col_edge[0 if g < RIM // 2 else 1]
                scale = edge if scale is None else scale * edge
            if scale is not None:
                accs[g] = accs[g] * scale
        return accs

    def spread_row(field, i):
        accs = [jnp.zeros((8, lanes), f32) for _ in range(cols // 2)]
        for a in range(TAPS):
            for b in range(TAPS):
                c = coef[a * TAPS + b]
                for g in range(cols // 2):
                    accs[g] = accs[g] + c * field[i + a, pl.ds(8 * g + b * PACK, 8), :]
        return accs

    for i in range(rows):
        loads[i].wait()
        for j in range(cols):
            f = i * cols + j
            flag = flag_ref[i, j].astype(f32)
            accs = [jnp.zeros((8, lanes), f32) for _ in range(tiles)]
            for k in range(blocks):
                z = jnp.broadcast_to(turned[k * 8 : (k + 1) * 8, f : f + 1], (8, lanes))
                for l in range(tiles):
                    accs[l] = accs[l] + z * jac[i, j, k * 8 : (k + 1) * 8, l * lanes : (l + 1) * lanes]
            store_part(0, i, j, [acc * flag for acc in accs])
        for d in range(n_chan - 1):
            chan_copy(0, i, d).start()
    finish_chan(0)
    start_rims(0)
    finish_rims(0)
    for e in range(ext_r):
        accs = spread_back_row(0, e)
        for g in range(pairs):
            fr[e, 8 * g : 8 * g + 8, :] = accs[g]
    finish_sends(0)

    def step(t, carry):
        par = lax.rem(t, 2)
        for i in range(rows):
            accs = spread_row(fr, i)
            for g in range(cols // 2):
                urs[i, 8 * g : 8 * g + 8, :] = accs[g]

            def column(j, carry):
                flag = flag_ref[i, j].astype(f32)
                x = [
                    jnp.broadcast_to(urs[i, pl.ds(j * PACK + l, 1), :] * flag, (8, lanes))
                    for l in range(tiles)
                ]
                accs = [jnp.zeros((8, lanes), f32) for _ in range(tiles)]
                for k in range(blocks):
                    js = [
                        jac[i, j, k * 8 : (k + 1) * 8, l * lanes : (l + 1) * lanes]
                        for l in range(tiles)
                    ]
                    y = js[0] * x[0]
                    for l in range(1, tiles):
                        y = y + js[l] * x[l]
                    z = jnp.sum(y, axis=1, keepdims=True) * wt[k]
                    for l in range(tiles):
                        accs[l] = accs[l] + js[l] * z
                store_part(par, i, j, accs)
                return carry

            lax.fori_loop(0, cols, column, 0, unroll=2)
            for d in range(n_chan - 1):
                chan_copy(par, i, d).start()

        norm_v = jnp.zeros((8, lanes), f32)
        for i in range(rows):
            for g in range(cols // 2):
                r = fr[RIM + i, 8 * g + RIM * PACK : 8 * g + RIM * PACK + 8, :]
                norm_v = norm_v + r * r
        finish_chan(par)
        start_rims(par)
        prod_v = norm_v
        for i in range(rows):
            for g in range(cols // 2):
                q = wide[par, WIDE + i, pl.ds(8 * g + WIDE * PACK, 8), :]
                prod_v = prod_v + urs[i, 8 * g : 8 * g + 8, :] * (
                    q
                )
        sums[par, g_me, 0:1, :] = jnp.sum(norm_v, axis=0, keepdims=True)
        sums[par, g_me, 1:2, :] = jnp.sum(prod_v, axis=0, keepdims=True)
        for d in range(group - 1):
            sum_copy(par, d).start()
        for d in range(group - 1):
            sum_copy(par, d).wait_recv()
        both = sums[par, 0]
        for n in range(1, group):
            both = both + sums[par, n]
        both = jnp.sum(both, axis=1, keepdims=True)
        fresh = jnp.broadcast_to(both[0:1], (8, lanes))
        product = jnp.broadcast_to(both[1:2], (8, lanes))
        beta = jnp.where(t == 1, zero, one) * (fresh / keep[0])
        alpha = fresh / (product - beta * fresh / keep[1])
        keep[0] = fresh
        keep[1] = alpha

        finish_rims(par)
        for e in range(ext_r):
            accs = spread_back_row(par, e)
            for g in range(pairs):
                at = slice(8 * g, 8 * g + 8)
                r = fr[e, at, :]
                d = r + beta * fd[e, at, :]
                c = (r + accs[g]) + beta * fc[e, at, :]
                fd[e, at, :] = d
                fc[e, at, :] = c
                fx[e, at, :] = fx[e, at, :] + alpha * d
                fr[e, at, :] = r - alpha * c
        finish_sends(par)
        for d in range(group - 1):
            sum_copy(par, d).wait_send()
        return carry

    lax.fori_loop(1, ITERS + 1, step, 0)

    for i in range(rows):
        accs = spread_row(fx, i)
        for g in range(cols // 2):
            urs[i, 8 * g : 8 * g + 8, :] = accs[g]
        for l in range(tiles):
            at = slice(l * lanes, (l + 1) * lanes)
            own = pl.ds(RIM * PACK + l, cols, stride=PACK)
            ctl_ref[i, :, at] = fx[RIM + i, own, :]
            res_ref[i, :, at] = fr[RIM + i, own, :]
            inc_ref[i, :, at] = urs[i, pl.ds(l, cols, stride=PACK), :]


def on_device(dims, jacobian, departures, inv_variance, channel_use, clear_flags, coefficients):
    rows, cols, chans, state = jacobian.shape
    lanes = 128
    n_along, n_across, n_chan = dims
    ext_r, ext_c = rows + 2 * RIM, cols + 2 * RIM
    field = jax.ShapeDtypeStruct((rows, cols, state), jnp.float32)
    vmem = pl.BlockSpec(memory_space=pltpu.VMEM)
    ext = pltpu.VMEM((ext_r, ext_c * PACK, lanes), jnp.float32)
    group = n_along * n_across
    return pl.pallas_call(
        functools.partial(kernel, dims),
        out_shape=(field, field, field),
        in_specs=[
            pl.BlockSpec(memory_space=pl.ANY), vmem, vmem, vmem,
            pl.BlockSpec(memory_space=pltpu.SMEM), vmem,
        ],
        out_specs=(vmem, vmem, vmem),
        scratch_shapes=[
            pltpu.VMEM((rows, cols, chans, state), jnp.float32),
            pltpu.VMEM((chans // 8, 8, lanes), jnp.float32),
            pltpu.VMEM((TAPS * TAPS, 8, lanes), jnp.float32),
            pltpu.VMEM((2, n_chan, rows * state // lanes * cols, lanes), jnp.float32),
            pltpu.VMEM((2, rows + 2 * WIDE, (cols + 2 * WIDE) * PACK, lanes), jnp.float32),
            pltpu.VMEM((2, group, 8, lanes), jnp.float32),
            pltpu.VMEM((rows, cols * PACK, lanes), jnp.float32),
            ext, ext, ext, ext,
            pltpu.VMEM((2, 8, lanes), jnp.float32),
            pltpu.SemaphoreType.DMA((rows,)),
            pltpu.SemaphoreType.DMA((2, rows, n_chan)),
            pltpu.SemaphoreType.DMA((2, rows, n_chan)),
            pltpu.SemaphoreType.DMA((2, 8)),
            pltpu.SemaphoreType.DMA((2, 8)),
            pltpu.SemaphoreType.DMA((2, group)),
            pltpu.SemaphoreType.DMA((2, group)),
        ],
        compiler_params=pltpu.CompilerParams(
            collective_id=0, has_side_effects=True, vmem_limit_bytes=40 * 1024 * 1024
        ),
    )(
        jacobian, departures, inv_variance.reshape(1, chans), channel_use.reshape(1, chans),
        clear_flags, coefficients,
    )


def solution(mesh):
    dims = (mesh.shape["along"], mesh.shape["across"], mesh.shape["chan"])
    return jax.shard_map(
        functools.partial(on_device, dims),
        mesh=mesh,
        in_specs=(
            P("along", "across", "chan", None),
            P("along", "across", "chan"),
            P("chan"),
            P("chan"),
            P("along", "across"),
            P(),
        ),
        out_specs=(
            P("along", "across", None),
            P("along", "across", None),
            P("along", "across", None),
        ),
        check_vma=False,
    )
```

```python
import functools

import jax
import jax.numpy as jnp
from jax import lax
from jax.experimental import pallas as pl
from jax.experimental.pallas import tpu as pltpu
from jax.sharding import PartitionSpec as P

ITERS = 10
RIM = 2
WIDE = 2 * RIM
TAPS = 2 * RIM + 1
PACK = 4
MESH = pl.DeviceIdType.MESH


def kernel(
    dims, jac_hbm, dep_ref, var_ref, use_ref, flag_ref, coef_ref,
    ctl_ref, inc_ref, res_ref,
    jac, wt, coef, part, wide, sums, urs, fr, fd, fc, fx, keep,
    jac_sem, chan_send, chan_recv, rim_send, rim_recv, sum_send, sum_recv,
):
    n_along, n_across, n_chan = dims
    rows, cols, chans, _ = jac.shape
    lanes = part.shape[-1]
    tiles = coef_ref.shape[1] // lanes
    ext_r, ext_c = rows + 2 * RIM, cols + 2 * RIM
    group = n_along * n_across
    f32 = jnp.float32

    a_me = lax.axis_index("along")
    x_me = lax.axis_index("across")
    c_me = lax.axis_index("chan")
    g_me = a_me * n_across + x_me

    loads = [
        pltpu.make_async_copy(jac_hbm.at[i], jac.at[i], jac_sem.at[i]) for i in range(rows)
    ]
    for load in loads:
        load.start()

    wide[...] = jnp.zeros_like(wide)
    sums[...] = jnp.zeros_like(sums)
    urs[...] = jnp.zeros_like(urs)
    fd[...] = jnp.zeros_like(fd)
    fc[...] = jnp.zeros_like(fc)
    fx[...] = jnp.zeros_like(fx)
    coef[...] = jnp.zeros_like(coef)
    keep[...] = jnp.ones_like(keep)

    chan_peers = [lax.rem(c_me + d, n_chan) for d in range(1, n_chan)]
    group_peers = []
    for d in range(1, group):
        peer = lax.rem(g_me + d, group)
        group_peers.append((peer // n_across, lax.rem(peer, n_across)))

    barrier = pltpu.get_barrier_semaphore()
    for c in chan_peers:
        pl.semaphore_signal(barrier, inc=1, device_id={"chan": c}, device_id_type=MESH)
    for a, x in group_peers:
        pl.semaphore_signal(
            barrier, inc=1, device_id={"along": a, "across": x}, device_id_type=MESH
        )
    pl.semaphore_wait(barrier, len(chan_peers) + len(group_peers))

    for t in range(TAPS * TAPS):
        for l in range(tiles):
            row = coef_ref[t : t + 1, l * lanes : (l + 1) * lanes]
            coef[t, l : l + 1, :] = row
            coef[t, PACK + l : PACK + l + 1, :] = row

    chan_weight = var_ref[...] * use_ref[...].astype(f32)
    wd = dep_ref[...].reshape(rows * cols, chans) * chan_weight
    stack = jnp.concatenate([wd, jnp.broadcast_to(chan_weight, (8, chans))], axis=0)
    turned = jnp.transpose(stack)
    blocks = chans // 8
    for k in range(blocks):
        wt[k] = jnp.broadcast_to(
            turned[k * 8 : (k + 1) * 8, rows * cols : rows * cols + 1], (8, lanes)
        )

    def chan_copy(par, i, d):
        place = part.at[par, c_me, pl.ds(i * tiles * cols, tiles * cols)]
        return pltpu.make_async_remote_copy(
            src_ref=place, dst_ref=place,
            send_sem=chan_send.at[par, i, d], recv_sem=chan_recv.at[par, i, d],
            device_id={"chan": chan_peers[d]}, device_id_type=MESH,
        )

    def store_part(par, i, j, accs):
        for l in range(tiles):
            part[par, c_me, pl.ds((i * tiles + l) * cols + j, 1), :] = jnp.sum(
                accs[l], axis=0, keepdims=True
            )

    sides = []
    for da in (-1, 0, 1):
        for dx in (-1, 0, 1):
            if da == 0 and dx == 0:
                continue
            here = None
            for delta, me, count in ((da, a_me, n_along), (dx, x_me, n_across)):
                if delta:
                    ok = me > 0 if delta < 0 else me < count - 1
                    here = ok if here is None else jnp.logical_and(here, ok)
            if da and n_along == 1 or dx and n_across == 1:
                continue

            def span(delta, size):
                if delta == 0:
                    return WIDE, size, WIDE
                if delta < 0:
                    return WIDE, WIDE, WIDE + size
                return size, WIDE, 0

            sides.append((da, dx, here, span(da, rows), span(dx, cols)))

    def rim_copy(par, n, k):
        da, dx, _, (r0, rn, rt), (c0, cn, ct) = sides[n]
        return pltpu.make_async_remote_copy(
            src_ref=wide.at[par, r0 + k, pl.ds(c0 * PACK, cn * PACK)],
            dst_ref=wide.at[par, rt + k, pl.ds(ct * PACK, cn * PACK)],
            send_sem=rim_send.at[par, n, k], recv_sem=rim_recv.at[par, n, k],
            device_id={"along": a_me + da, "across": x_me + dx}, device_id_type=MESH,
        )

    opposite = {
        n: next(m for m, t in enumerate(sides) if (t[0], t[1]) == (-s[0], -s[1]))
        for n, s in enumerate(sides)
    }

    def sum_copy(par, d):
        a, x = group_peers[d]
        place = sums.at[par, g_me]
        return pltpu.make_async_remote_copy(
            src_ref=place, dst_ref=place,
            send_sem=sum_send.at[par, d], recv_sem=sum_recv.at[par, d],
            device_id={"along": a, "across": x}, device_id_type=MESH,
        )

    def finish_chan(par):
        for i in range(rows):
            for d in range(n_chan - 1):
                chan_copy(par, i, d).wait_recv()
            for l in range(tiles):
                at = pl.ds((i * tiles + l) * cols, cols)
                total = part[par, 0, at, :]
                for c in range(1, n_chan):
                    total = total + part[par, c, at, :]
                wide[par, WIDE + i, pl.ds(WIDE * PACK + l, cols, stride=PACK), :] = total
            for n, side in enumerate(sides):
                k = WIDE + i - side[3][0]
                if 0 <= k < side[3][1]:
                    @pl.when(side[2])
                    def _():
                        rim_copy(par, n, k).start()

    def finish_rims(par):
        for n, side in enumerate(sides):
            @pl.when(side[2])
            def _():
                for k in range(sides[opposite[n]][3][1]):
                    rim_copy(par, opposite[n], k).wait_recv()

    def finish_sends(par):
        for i in range(rows):
            for d in range(n_chan - 1):
                chan_copy(par, i, d).wait_send()
        for n, side in enumerate(sides):
            @pl.when(side[2])
            def _():
                for k in range(side[3][1]):
                    rim_copy(par, n, k).wait_send()

    one, zero = jnp.float32(1), jnp.float32(0)
    row_edge = (
        jnp.where(a_me > 0, one, zero), jnp.where(a_me < n_along - 1, one, zero)
    )
    col_edge = (
        jnp.where(x_me > 0, one, zero), jnp.where(x_me < n_across - 1, one, zero)
    )
    pairs = ext_c // 2

    def spread_back_row(par, e):
        accs = [jnp.zeros((8, lanes), f32) for _ in range(pairs)]
        for a in range(TAPS):
            for b in range(TAPS):
                c = coef[a * TAPS + b]
                for g in range(pairs):
                    accs[g] = accs[g] + c * wide[
                        par, e + WIDE - a, pl.ds(8 * g + (WIDE - b) * PACK, 8), :
                    ]
        for g in range(pairs):
            scale = None
            if e < RIM or e >= RIM + rows:
                scale = row_edge[0 if e < RIM else 1]
            if g < RIM // 2 or g >= (RIM + cols) // 2:
                edge = col_edge[0 if g < RIM // 2 else 1]
                scale = edge if scale is None else scale * edge
            if scale is not None:
                accs[g] = accs[g] * scale
        return accs

    def spread_row(field, i):
        accs = [jnp.zeros((8, lanes), f32) for _ in range(cols // 2)]
        for a in range(TAPS):
            for b in range(TAPS):
                c = coef[a * TAPS + b]
                for g in range(cols // 2):
                    accs[g] = accs[g] + c * field[i + a, pl.ds(8 * g + b * PACK, 8), :]
        return accs

    for i in range(rows):
        loads[i].wait()
        for j in range(cols):
            f = i * cols + j
            flag = flag_ref[i, j].astype(f32)
            accs = [jnp.zeros((8, lanes), f32) for _ in range(tiles)]
            for k in range(blocks):
                z = jnp.broadcast_to(turned[k * 8 : (k + 1) * 8, f : f + 1], (8, lanes))
                for l in range(tiles):
                    accs[l] = accs[l] + z * jac[i, j, k * 8 : (k + 1) * 8, l * lanes : (l + 1) * lanes]
            store_part(0, i, j, [acc * flag for acc in accs])
        for d in range(n_chan - 1):
            chan_copy(0, i, d).start()
    finish_chan(0)
    finish_rims(0)
    for e in range(ext_r):
        accs = spread_back_row(0, e)
        for g in range(pairs):
            fr[e, 8 * g : 8 * g + 8, :] = accs[g]
    finish_sends(0)

    def step(t, carry):
        par = lax.rem(t, 2)
        for i in range(rows):
            accs = spread_row(fr, i)
            for g in range(cols // 2):
                urs[i, 8 * g : 8 * g + 8, :] = accs[g]

            def column(j, carry):
                flag = flag_ref[i, j].astype(f32)
                x = [
                    jnp.broadcast_to(urs[i, pl.ds(j * PACK + l, 1), :] * flag, (8, lanes))
                    for l in range(tiles)
                ]
                accs = [jnp.zeros((8, lanes), f32) for _ in range(tiles)]
                for k in range(blocks):
                    js = [
                        jac[i, j, k * 8 : (k + 1) * 8, l * lanes : (l + 1) * lanes]
                        for l in range(tiles)
                    ]
                    y = js[0] * x[0]
                    for l in range(1, tiles):
                        y = y + js[l] * x[l]
                    z = jnp.sum(y, axis=1, keepdims=True) * wt[k]
                    for l in range(tiles):
                        accs[l] = accs[l] + js[l] * z
                store_part(par, i, j, accs)
                return carry

            lax.fori_loop(0, cols, column, 0, unroll=2)
            for d in range(n_chan - 1):
                chan_copy(par, i, d).start()

        norm_v = jnp.zeros((8, lanes), f32)
        for i in range(rows):
            for g in range(cols // 2):
                r = fr[RIM + i, 8 * g + RIM * PACK : 8 * g + RIM * PACK + 8, :]
                norm_v = norm_v + r * r
        finish_chan(par)
        prod_v = norm_v
        for i in range(rows):
            for g in range(cols // 2):
                q = wide[par, WIDE + i, pl.ds(8 * g + WIDE * PACK, 8), :]
                prod_v = prod_v + urs[i, 8 * g : 8 * g + 8, :] * (
                    q
                )
        sums[par, g_me, 0:1, :] = jnp.sum(norm_v, axis=0, keepdims=True)
        sums[par, g_me, 1:2, :] = jnp.sum(prod_v, axis=0, keepdims=True)
        for d in range(group - 1):
            sum_copy(par, d).start()
        for d in range(group - 1):
            sum_copy(par, d).wait_recv()
        both = sums[par, 0]
        for n in range(1, group):
            both = both + sums[par, n]
        both = jnp.sum(both, axis=1, keepdims=True)
        fresh = jnp.broadcast_to(both[0:1], (8, lanes))
        product = jnp.broadcast_to(both[1:2], (8, lanes))
        beta = jnp.where(t == 1, zero, one) * (fresh / keep[0])
        alpha = fresh / (product - beta * fresh / keep[1])
        keep[0] = fresh
        keep[1] = alpha

        finish_rims(par)
        for e in range(ext_r):
            accs = spread_back_row(par, e)
            for g in range(pairs):
                at = slice(8 * g, 8 * g + 8)
                r = fr[e, at, :]
                d = r + beta * fd[e, at, :]
                c = (r + accs[g]) + beta * fc[e, at, :]
                fd[e, at, :] = d
                fc[e, at, :] = c
                fx[e, at, :] = fx[e, at, :] + alpha * d
                fr[e, at, :] = r - alpha * c
        finish_sends(par)
        for d in range(group - 1):
            sum_copy(par, d).wait_send()
        return carry

    lax.fori_loop(1, ITERS + 1, step, 0)

    for i in range(rows):
        accs = spread_row(fx, i)
        for g in range(cols // 2):
            urs[i, 8 * g : 8 * g + 8, :] = accs[g]
        for l in range(tiles):
            at = slice(l * lanes, (l + 1) * lanes)
            own = pl.ds(RIM * PACK + l, cols, stride=PACK)
            ctl_ref[i, :, at] = fx[RIM + i, own, :]
            res_ref[i, :, at] = fr[RIM + i, own, :]
            inc_ref[i, :, at] = urs[i, pl.ds(l, cols, stride=PACK), :]


def on_device(dims, jacobian, departures, inv_variance, channel_use, clear_flags, coefficients):
    rows, cols, chans, state = jacobian.shape
    lanes = 128
    n_along, n_across, n_chan = dims
    ext_r, ext_c = rows + 2 * RIM, cols + 2 * RIM
    field = jax.ShapeDtypeStruct((rows, cols, state), jnp.float32)
    vmem = pl.BlockSpec(memory_space=pltpu.VMEM)
    ext = pltpu.VMEM((ext_r, ext_c * PACK, lanes), jnp.float32)
    group = n_along * n_across
    return pl.pallas_call(
        functools.partial(kernel, dims),
        out_shape=(field, field, field),
        in_specs=[
            pl.BlockSpec(memory_space=pl.ANY), vmem, vmem, vmem,
            pl.BlockSpec(memory_space=pltpu.SMEM), vmem,
        ],
        out_specs=(vmem, vmem, vmem),
        scratch_shapes=[
            pltpu.VMEM((rows, cols, chans, state), jnp.float32),
            pltpu.VMEM((chans // 8, 8, lanes), jnp.float32),
            pltpu.VMEM((TAPS * TAPS, 8, lanes), jnp.float32),
            pltpu.VMEM((2, n_chan, rows * state // lanes * cols, lanes), jnp.float32),
            pltpu.VMEM((2, rows + 2 * WIDE, (cols + 2 * WIDE) * PACK, lanes), jnp.float32),
            pltpu.VMEM((2, group, 8, lanes), jnp.float32),
            pltpu.VMEM((rows, cols * PACK, lanes), jnp.float32),
            ext, ext, ext, ext,
            pltpu.VMEM((2, 8, lanes), jnp.float32),
            pltpu.SemaphoreType.DMA((rows,)),
            pltpu.SemaphoreType.DMA((2, rows, n_chan)),
            pltpu.SemaphoreType.DMA((2, rows, n_chan)),
            pltpu.SemaphoreType.DMA((2, 8, max(rows, WIDE))),
            pltpu.SemaphoreType.DMA((2, 8, max(rows, WIDE))),
            pltpu.SemaphoreType.DMA((2, group)),
            pltpu.SemaphoreType.DMA((2, group)),
        ],
        compiler_params=pltpu.CompilerParams(
            collective_id=0, has_side_effects=True, vmem_limit_bytes=60 * 1024 * 1024
        ),
    )(
        jacobian, departures, inv_variance.reshape(1, chans), channel_use.reshape(1, chans),
        clear_flags, coefficients,
    )


def solution(mesh):
    dims = (mesh.shape["along"], mesh.shape["across"], mesh.shape["chan"])
    return jax.shard_map(
        functools.partial(on_device, dims),
        mesh=mesh,
        in_specs=(
            P("along", "across", "chan", None),
            P("along", "across", "chan"),
            P("chan"),
            P("chan"),
            P("along", "across"),
            P(),
        ),
        out_specs=(
            P("along", "across", None),
            P("along", "across", None),
            P("along", "across", None),
        ),
        check_vma=False,
    )
```

```python
import functools

import jax
import jax.numpy as jnp
from jax import lax
from jax.experimental import pallas as pl
from jax.experimental.pallas import tpu as pltpu
from jax.sharding import PartitionSpec as P

ITERS = 10
RIM = 2
WIDE = 2 * RIM
TAPS = 2 * RIM + 1
PACK = 4
MESH = pl.DeviceIdType.MESH


def kernel(
    dims, jac_hbm, dep_ref, var_ref, use_ref, flag_ref, coef_ref,
    ctl_ref, inc_ref, res_ref,
    jac, wt, coef, part, wide, sums, urs, image, fr, fd, fc, fx, keep,
    jac_sem, chan_send, chan_recv, rim_send, rim_recv, sum_send, sum_recv,
):
    n_along, n_across, n_chan = dims
    rows, cols, chans, _ = jac.shape
    lanes = part.shape[-1]
    tiles = coef_ref.shape[1] // lanes
    ext_r, ext_c = rows + 2 * RIM, cols + 2 * RIM
    group = n_along * n_across
    f32 = jnp.float32

    a_me = lax.axis_index("along")
    x_me = lax.axis_index("across")
    c_me = lax.axis_index("chan")
    g_me = a_me * n_across + x_me

    loads = [
        pltpu.make_async_copy(jac_hbm.at[i], jac.at[i], jac_sem.at[i]) for i in range(rows)
    ]
    for load in loads:
        load.start()

    wide[...] = jnp.zeros_like(wide)
    sums[...] = jnp.zeros_like(sums)
    urs[...] = jnp.zeros_like(urs)
    fd[...] = jnp.zeros_like(fd)
    fc[...] = jnp.zeros_like(fc)
    fx[...] = jnp.zeros_like(fx)
    coef[...] = jnp.zeros_like(coef)
    keep[...] = jnp.ones_like(keep)

    chan_peers = [lax.rem(c_me + d, n_chan) for d in range(1, n_chan)]
    group_peers = []
    for d in range(1, group):
        peer = lax.rem(g_me + d, group)
        group_peers.append((peer // n_across, lax.rem(peer, n_across)))

    barrier = pltpu.get_barrier_semaphore()
    for c in chan_peers:
        pl.semaphore_signal(barrier, inc=1, device_id={"chan": c}, device_id_type=MESH)
    for a, x in group_peers:
        pl.semaphore_signal(
            barrier, inc=1, device_id={"along": a, "across": x}, device_id_type=MESH
        )
    pl.semaphore_wait(barrier, len(chan_peers) + len(group_peers))

    for t in range(TAPS * TAPS):
        for l in range(tiles):
            row = coef_ref[t : t + 1, l * lanes : (l + 1) * lanes]
            coef[t, l : l + 1, :] = row
            coef[t, PACK + l : PACK + l + 1, :] = row

    chan_weight = var_ref[...] * use_ref[...].astype(f32)
    wd = dep_ref[...].reshape(rows * cols, chans) * chan_weight
    stack = jnp.concatenate([wd, jnp.broadcast_to(chan_weight, (8, chans))], axis=0)
    turned = jnp.transpose(stack)
    blocks = chans // 8
    for k in range(blocks):
        wt[k] = jnp.broadcast_to(
            turned[k * 8 : (k + 1) * 8, rows * cols : rows * cols + 1], (8, lanes)
        )

    def chan_copy(par, i, d):
        place = part.at[par, c_me, pl.ds(i * tiles * cols, tiles * cols)]
        return pltpu.make_async_remote_copy(
            src_ref=place, dst_ref=place,
            send_sem=chan_send.at[par, i, d], recv_sem=chan_recv.at[par, i, d],
            device_id={"chan": chan_peers[d]}, device_id_type=MESH,
        )

    def store_part(par, i, j, accs):
        for l in range(tiles):
            part[par, c_me, pl.ds((i * tiles + l) * cols + j, 1), :] = jnp.sum(
                accs[l], axis=0, keepdims=True
            )

    sides = []
    for da in (-1, 0, 1):
        for dx in (-1, 0, 1):
            if da == 0 and dx == 0:
                continue
            here = None
            for delta, me, count in ((da, a_me, n_along), (dx, x_me, n_across)):
                if delta:
                    ok = me > 0 if delta < 0 else me < count - 1
                    here = ok if here is None else jnp.logical_and(here, ok)
            if da and n_along == 1 or dx and n_across == 1:
                continue

            def span(delta, size):
                if delta == 0:
                    return WIDE, size, WIDE
                if delta < 0:
                    return WIDE, WIDE, WIDE + size
                return size, WIDE, 0

            sides.append((da, dx, here, span(da, rows), span(dx, cols)))

    def rim_copy(par, n, k):
        da, dx, _, (r0, rn, rt), (c0, cn, ct) = sides[n]
        return pltpu.make_async_remote_copy(
            src_ref=wide.at[par, r0 + k, pl.ds(c0 * PACK, cn * PACK)],
            dst_ref=wide.at[par, rt + k, pl.ds(ct * PACK, cn * PACK)],
            send_sem=rim_send.at[par, n, k], recv_sem=rim_recv.at[par, n, k],
            device_id={"along": a_me + da, "across": x_me + dx}, device_id_type=MESH,
        )

    opposite = {
        n: next(m for m, t in enumerate(sides) if (t[0], t[1]) == (-s[0], -s[1]))
        for n, s in enumerate(sides)
    }

    def sum_copy(par, d):
        a, x = group_peers[d]
        place = sums.at[par, g_me]
        return pltpu.make_async_remote_copy(
            src_ref=place, dst_ref=place,
            send_sem=sum_send.at[par, d], recv_sem=sum_recv.at[par, d],
            device_id={"along": a, "across": x}, device_id_type=MESH,
        )

    def finish_chan(par):
        for i in range(rows):
            for d in range(n_chan - 1):
                chan_copy(par, i, d).wait_recv()
            for l in range(tiles):
                at = pl.ds((i * tiles + l) * cols, cols)
                total = part[par, 0, at, :]
                for c in range(1, n_chan):
                    total = total + part[par, c, at, :]
                wide[par, WIDE + i, pl.ds(WIDE * PACK + l, cols, stride=PACK), :] = total
            for n, side in enumerate(sides):
                k = WIDE + i - side[3][0]
                if 0 <= k < side[3][1]:
                    @pl.when(side[2])
                    def _():
                        rim_copy(par, n, k).start()

    def finish_rims(par):
        for n, side in enumerate(sides):
            @pl.when(side[2])
            def _():
                for k in range(sides[opposite[n]][3][1]):
                    rim_copy(par, opposite[n], k).wait_recv()

    def finish_sends(par):
        for i in range(rows):
            for d in range(n_chan - 1):
                chan_copy(par, i, d).wait_send()
        for n, side in enumerate(sides):
            @pl.when(side[2])
            def _():
                for k in range(side[3][1]):
                    rim_copy(par, n, k).wait_send()

    one, zero = jnp.float32(1), jnp.float32(0)
    row_edge = (
        jnp.where(a_me > 0, one, zero), jnp.where(a_me < n_along - 1, one, zero)
    )
    col_edge = (
        jnp.where(x_me > 0, one, zero), jnp.where(x_me < n_across - 1, one, zero)
    )
    pairs = ext_c // 2

    def spread_back_row(par, e):
        accs = [jnp.zeros((8, lanes), f32) for _ in range(pairs)]
        for a in range(TAPS):
            for b in range(TAPS):
                c = coef[a * TAPS + b]
                for g in range(pairs):
                    accs[g] = accs[g] + c * wide[
                        par, e + WIDE - a, pl.ds(8 * g + (WIDE - b) * PACK, 8), :
                    ]
        for g in range(pairs):
            scale = None
            if e < RIM or e >= RIM + rows:
                scale = row_edge[0 if e < RIM else 1]
            if g < RIM // 2 or g >= (RIM + cols) // 2:
                edge = col_edge[0 if g < RIM // 2 else 1]
                scale = edge if scale is None else scale * edge
            if scale is not None:
                accs[g] = accs[g] * scale
        return accs

    def spread_row(field, i):
        accs = [jnp.zeros((8, lanes), f32) for _ in range(cols // 2)]
        for a in range(TAPS):
            for b in range(TAPS):
                c = coef[a * TAPS + b]
                for g in range(cols // 2):
                    accs[g] = accs[g] + c * field[i + a, pl.ds(8 * g + b * PACK, 8), :]
        return accs

    for i in range(rows):
        loads[i].wait()
        for j in range(cols):
            f = i * cols + j
            flag = flag_ref[i, j].astype(f32)
            accs = [jnp.zeros((8, lanes), f32) for _ in range(tiles)]
            for k in range(blocks):
                z = jnp.broadcast_to(turned[k * 8 : (k + 1) * 8, f : f + 1], (8, lanes))
                for l in range(tiles):
                    accs[l] = accs[l] + z * jac[i, j, k * 8 : (k + 1) * 8, l * lanes : (l + 1) * lanes]
            store_part(0, i, j, [acc * flag for acc in accs])
        for d in range(n_chan - 1):
            chan_copy(0, i, d).start()
    finish_chan(0)
    finish_rims(0)
    for e in range(ext_r):
        accs = spread_back_row(0, e)
        for g in range(pairs):
            fr[e, 8 * g : 8 * g + 8, :] = accs[g]
    finish_sends(0)

    def step(t, carry):
        par = lax.rem(t, 2)
        for i in range(rows):
            accs = spread_row(fr, i)
            for g in range(cols // 2):
                urs[i, 8 * g : 8 * g + 8, :] = accs[g]

            def column(j, carry):
                flag = flag_ref[i, j].astype(f32)
                x = [
                    jnp.broadcast_to(urs[i, pl.ds(j * PACK + l, 1), :] * flag, (8, lanes))
                    for l in range(tiles)
                ]
                accs = [jnp.zeros((8, lanes), f32) for _ in range(tiles)]
                for k in range(blocks):
                    js = [
                        jac[i, j, k * 8 : (k + 1) * 8, l * lanes : (l + 1) * lanes]
                        for l in range(tiles)
                    ]
                    y = js[0] * x[0]
                    for l in range(1, tiles):
                        y = y + js[l] * x[l]
                    z = jnp.sum(y, axis=1, keepdims=True) * wt[k]
                    for l in range(tiles):
                        accs[l] = accs[l] + js[l] * z
                store_part(par, i, j, accs)
                return carry

            lax.fori_loop(0, cols, column, 0, unroll=8)
            for d in range(n_chan - 1):
                chan_copy(par, i, d).start()

        norm_v = jnp.zeros((8, lanes), f32)
        for i in range(rows):
            for g in range(cols // 2):
                r = fr[RIM + i, 8 * g + RIM * PACK : 8 * g + RIM * PACK + 8, :]
                norm_v = norm_v + r * r
        finish_chan(par)
        prod_v = norm_v
        for i in range(rows):
            for g in range(cols // 2):
                q = wide[par, WIDE + i, pl.ds(8 * g + WIDE * PACK, 8), :]
                prod_v = prod_v + urs[i, 8 * g : 8 * g + 8, :] * q
        sums[par, g_me, 0:1, :] = jnp.sum(norm_v, axis=0, keepdims=True)
        sums[par, g_me, 1:2, :] = jnp.sum(prod_v, axis=0, keepdims=True)
        for d in range(group - 1):
            sum_copy(par, d).start()
        finish_rims(par)
        for d in range(group - 1):
            sum_copy(par, d).wait_recv()
        for e in range(ext_r):
            accs = spread_back_row(par, e)
            for g in range(pairs):
                image[e, 8 * g : 8 * g + 8, :] = accs[g]
        both = sums[par, 0]
        for n in range(1, group):
            both = both + sums[par, n]
        both = jnp.sum(both, axis=1, keepdims=True)
        fresh = jnp.broadcast_to(both[0:1], (8, lanes))
        product = jnp.broadcast_to(both[1:2], (8, lanes))
        beta = jnp.where(t == 1, zero, one) * (fresh / keep[0])
        alpha = fresh / (product - beta * fresh / keep[1])
        keep[0] = fresh
        keep[1] = alpha

        for e in range(ext_r):
            for g in range(pairs):
                at = slice(8 * g, 8 * g + 8)
                r = fr[e, at, :]
                d = r + beta * fd[e, at, :]
                c = (r + image[e, at, :]) + beta * fc[e, at, :]
                fd[e, at, :] = d
                fc[e, at, :] = c
                fx[e, at, :] = fx[e, at, :] + alpha * d
                fr[e, at, :] = r - alpha * c
        finish_sends(par)
        for d in range(group - 1):
            sum_copy(par, d).wait_send()
        return carry

    lax.fori_loop(1, ITERS + 1, step, 0)

    for i in range(rows):
        accs = spread_row(fx, i)
        for g in range(cols // 2):
            urs[i, 8 * g : 8 * g + 8, :] = accs[g]
        for l in range(tiles):
            at = slice(l * lanes, (l + 1) * lanes)
            own = pl.ds(RIM * PACK + l, cols, stride=PACK)
            ctl_ref[i, :, at] = fx[RIM + i, own, :]
            res_ref[i, :, at] = fr[RIM + i, own, :]
            inc_ref[i, :, at] = urs[i, pl.ds(l, cols, stride=PACK), :]


def on_device(dims, jacobian, departures, inv_variance, channel_use, clear_flags, coefficients):
    rows, cols, chans, state = jacobian.shape
    lanes = 128
    n_along, n_across, n_chan = dims
    ext_r, ext_c = rows + 2 * RIM, cols + 2 * RIM
    field = jax.ShapeDtypeStruct((rows, cols, state), jnp.float32)
    vmem = pl.BlockSpec(memory_space=pltpu.VMEM)
    ext = pltpu.VMEM((ext_r, ext_c * PACK, lanes), jnp.float32)
    group = n_along * n_across
    return pl.pallas_call(
        functools.partial(kernel, dims),
        out_shape=(field, field, field),
        in_specs=[
            pl.BlockSpec(memory_space=pl.ANY), vmem, vmem, vmem,
            pl.BlockSpec(memory_space=pltpu.SMEM), vmem,
        ],
        out_specs=(vmem, vmem, vmem),
        scratch_shapes=[
            pltpu.VMEM((rows, cols, chans, state), jnp.float32),
            pltpu.VMEM((chans // 8, 8, lanes), jnp.float32),
            pltpu.VMEM((TAPS * TAPS, 8, lanes), jnp.float32),
            pltpu.VMEM((2, n_chan, rows * state // lanes * cols, lanes), jnp.float32),
            pltpu.VMEM((2, rows + 2 * WIDE, (cols + 2 * WIDE) * PACK, lanes), jnp.float32),
            pltpu.VMEM((2, group, 8, lanes), jnp.float32),
            pltpu.VMEM((rows, cols * PACK, lanes), jnp.float32),
            ext, ext, ext, ext, ext,
            pltpu.VMEM((2, 8, lanes), jnp.float32),
            pltpu.SemaphoreType.DMA((rows,)),
            pltpu.SemaphoreType.DMA((2, rows, n_chan)),
            pltpu.SemaphoreType.DMA((2, rows, n_chan)),
            pltpu.SemaphoreType.DMA((2, 8, max(rows, WIDE))),
            pltpu.SemaphoreType.DMA((2, 8, max(rows, WIDE))),
            pltpu.SemaphoreType.DMA((2, group)),
            pltpu.SemaphoreType.DMA((2, group)),
        ],
        compiler_params=pltpu.CompilerParams(
            collective_id=0, has_side_effects=True, vmem_limit_bytes=60 * 1024 * 1024
        ),
    )(
        jacobian, departures, inv_variance.reshape(1, chans), channel_use.reshape(1, chans),
        clear_flags, coefficients,
    )


def solution(mesh):
    dims = (mesh.shape["along"], mesh.shape["across"], mesh.shape["chan"])
    return jax.shard_map(
        functools.partial(on_device, dims),
        mesh=mesh,
        in_specs=(
            P("along", "across", "chan", None),
            P("along", "across", "chan"),
            P("chan"),
            P("chan"),
            P("along", "across"),
            P(),
        ),
        out_specs=(
            P("along", "across", None),
            P("along", "across", None),
            P("along", "across", None),
        ),
        check_vma=False,
    )
```

```python
import functools

import jax
import jax.numpy as jnp
from jax import lax
from jax.experimental import pallas as pl
from jax.experimental.pallas import tpu as pltpu
from jax.sharding import PartitionSpec as P

ITERS = 10
RIM = 2
WIDE = 2 * RIM
TAPS = 2 * RIM + 1
PACK = 4
MESH = pl.DeviceIdType.MESH


def kernel(
    dims, jac_hbm, dep_ref, var_ref, use_ref, flag_ref, coef_ref,
    ctl_ref, inc_ref, res_ref,
    jac, wt, coef, part, wide, sums, urs, image, fr, fd, fc, fx, keep,
    jac_sem, chan_send, chan_recv, rim_send, rim_recv, sum_send, sum_recv,
):
    n_along, n_across, n_chan = dims
    rows, cols, chans, _ = jac.shape
    lanes = part.shape[-1]
    tiles = coef_ref.shape[1] // lanes
    ext_r, ext_c = rows + 2 * RIM, cols + 2 * RIM
    group = n_along * n_across
    f32 = jnp.float32

    a_me = lax.axis_index("along")
    x_me = lax.axis_index("across")
    c_me = lax.axis_index("chan")
    g_me = a_me * n_across + x_me

    loads = [
        pltpu.make_async_copy(jac_hbm.at[i], jac.at[i], jac_sem.at[i]) for i in range(rows)
    ]
    for load in loads:
        load.start()

    wide[...] = jnp.zeros_like(wide)
    sums[...] = jnp.zeros_like(sums)
    urs[...] = jnp.zeros_like(urs)
    fd[...] = jnp.zeros_like(fd)
    fc[...] = jnp.zeros_like(fc)
    fx[...] = jnp.zeros_like(fx)
    coef[...] = jnp.zeros_like(coef)
    keep[...] = jnp.ones_like(keep)

    steps = sorted(range(1, n_chan), key=lambda d: -min(d, n_chan - d))
    chan_peers = [lax.rem(c_me + d, n_chan) for d in steps]
    group_peers = []
    for d in range(1, group):
        peer = lax.rem(g_me + d, group)
        group_peers.append((peer // n_across, lax.rem(peer, n_across)))

    barrier = pltpu.get_barrier_semaphore()
    for c in chan_peers:
        pl.semaphore_signal(barrier, inc=1, device_id={"chan": c}, device_id_type=MESH)
    for a, x in group_peers:
        pl.semaphore_signal(
            barrier, inc=1, device_id={"along": a, "across": x}, device_id_type=MESH
        )
    pl.semaphore_wait(barrier, len(chan_peers) + len(group_peers))

    for t in range(TAPS * TAPS):
        for l in range(tiles):
            row = coef_ref[t : t + 1, l * lanes : (l + 1) * lanes]
            coef[t, l : l + 1, :] = row
            coef[t, PACK + l : PACK + l + 1, :] = row

    chan_weight = var_ref[...] * use_ref[...].astype(f32)
    wd = dep_ref[...].reshape(rows * cols, chans) * chan_weight
    stack = jnp.concatenate([wd, jnp.broadcast_to(chan_weight, (8, chans))], axis=0)
    turned = jnp.transpose(stack)
    blocks = chans // 8
    for k in range(blocks):
        wt[k] = jnp.broadcast_to(
            turned[k * 8 : (k + 1) * 8, rows * cols : rows * cols + 1], (8, lanes)
        )

    def chan_copy(par, i, d):
        place = part.at[par, c_me, pl.ds(i * tiles * cols, tiles * cols)]
        return pltpu.make_async_remote_copy(
            src_ref=place, dst_ref=place,
            send_sem=chan_send.at[par, i, d], recv_sem=chan_recv.at[par, i, d],
            device_id={"chan": chan_peers[d]}, device_id_type=MESH,
        )

    def store_part(par, i, j, accs):
        for l in range(tiles):
            part[par, c_me, pl.ds((i * tiles + l) * cols + j, 1), :] = jnp.sum(
                accs[l], axis=0, keepdims=True
            )

    sides = []
    for dx in (-1, 1, 0):
        for da in (-1, 0, 1):
            if da == 0 and dx == 0:
                continue
            here = None
            for delta, me, count in ((da, a_me, n_along), (dx, x_me, n_across)):
                if delta:
                    ok = me > 0 if delta < 0 else me < count - 1
                    here = ok if here is None else jnp.logical_and(here, ok)
            if da and n_along == 1 or dx and n_across == 1:
                continue

            def span(delta, size):
                if delta == 0:
                    return WIDE, size, WIDE
                if delta < 0:
                    return WIDE, WIDE, WIDE + size
                return size, WIDE, 0

            sides.append((da, dx, here, span(da, rows), span(dx, cols)))

    def rim_copy(par, n, k):
        da, dx, _, (r0, rn, rt), (c0, cn, ct) = sides[n]
        return pltpu.make_async_remote_copy(
            src_ref=wide.at[par, r0 + k, pl.ds(c0 * PACK, cn * PACK)],
            dst_ref=wide.at[par, rt + k, pl.ds(ct * PACK, cn * PACK)],
            send_sem=rim_send.at[par, n, k], recv_sem=rim_recv.at[par, n, k],
            device_id={"along": a_me + da, "across": x_me + dx}, device_id_type=MESH,
        )

    opposite = {
        n: next(m for m, t in enumerate(sides) if (t[0], t[1]) == (-s[0], -s[1]))
        for n, s in enumerate(sides)
    }

    def sum_copy(par, d):
        a, x = group_peers[d]
        place = sums.at[par, g_me]
        return pltpu.make_async_remote_copy(
            src_ref=place, dst_ref=place,
            send_sem=sum_send.at[par, d], recv_sem=sum_recv.at[par, d],
            device_id={"along": a, "across": x}, device_id_type=MESH,
        )

    def finish_chan(par):
        for i in range(rows):
            for d in range(n_chan - 1):
                chan_copy(par, i, d).wait_recv()
            for l in range(tiles):
                at = pl.ds((i * tiles + l) * cols, cols)
                total = part[par, 0, at, :]
                for c in range(1, n_chan):
                    total = total + part[par, c, at, :]
                wide[par, WIDE + i, pl.ds(WIDE * PACK + l, cols, stride=PACK), :] = total
            for n, side in enumerate(sides):
                k = WIDE + i - side[3][0]
                if 0 <= k < side[3][1]:
                    @pl.when(side[2])
                    def _():
                        rim_copy(par, n, k).start()

    def finish_rims(par):
        for n, side in enumerate(sides):
            @pl.when(side[2])
            def _():
                for k in range(sides[opposite[n]][3][1]):
                    rim_copy(par, opposite[n], k).wait_recv()

    def finish_sends(par):
        for i in range(rows):
            for d in range(n_chan - 1):
                chan_copy(par, i, d).wait_send()
        for n, side in enumerate(sides):
            @pl.when(side[2])
            def _():
                for k in range(side[3][1]):
                    rim_copy(par, n, k).wait_send()

    one, zero = jnp.float32(1), jnp.float32(0)
    row_edge = (
        jnp.where(a_me > 0, one, zero), jnp.where(a_me < n_along - 1, one, zero)
    )
    col_edge = (
        jnp.where(x_me > 0, one, zero), jnp.where(x_me < n_across - 1, one, zero)
    )
    pairs = ext_c // 2

    def spread_back_row(par, e):
        accs = [jnp.zeros((8, lanes), f32) for _ in range(pairs)]
        for a in range(TAPS):
            for b in range(TAPS):
                c = coef[a * TAPS + b]
                for g in range(pairs):
                    accs[g] = accs[g] + c * wide[
                        par, e + WIDE - a, pl.ds(8 * g + (WIDE - b) * PACK, 8), :
                    ]
        for g in range(pairs):
            scale = None
            if e < RIM or e >= RIM + rows:
                scale = row_edge[0 if e < RIM else 1]
            if g < RIM // 2 or g >= (RIM + cols) // 2:
                edge = col_edge[0 if g < RIM // 2 else 1]
                scale = edge if scale is None else scale * edge
            if scale is not None:
                accs[g] = accs[g] * scale
        return accs

    def spread_row(field, i):
        accs = [jnp.zeros((8, lanes), f32) for _ in range(cols // 2)]
        for a in range(TAPS):
            for b in range(TAPS):
                c = coef[a * TAPS + b]
                for g in range(cols // 2):
                    accs[g] = accs[g] + c * field[i + a, pl.ds(8 * g + b * PACK, 8), :]
        return accs

    for i in range(rows):
        loads[i].wait()
        for j in range(cols):
            f = i * cols + j
            flag = flag_ref[i, j].astype(f32)
            accs = [jnp.zeros((8, lanes), f32) for _ in range(tiles)]
            for k in range(blocks):
                z = jnp.broadcast_to(turned[k * 8 : (k + 1) * 8, f : f + 1], (8, lanes))
                for l in range(tiles):
                    accs[l] = accs[l] + z * jac[i, j, k * 8 : (k + 1) * 8, l * lanes : (l + 1) * lanes]
            store_part(0, i, j, [acc * flag for acc in accs])
        for d in range(n_chan - 1):
            chan_copy(0, i, d).start()
    finish_chan(0)
    finish_rims(0)
    for e in range(ext_r):
        accs = spread_back_row(0, e)
        for g in range(pairs):
            fr[e, 8 * g : 8 * g + 8, :] = accs[g]
    finish_sends(0)

    def step(t, carry):
        par = lax.rem(t, 2)
        for i in range(rows):
            accs = spread_row(fr, i)
            for g in range(cols // 2):
                urs[i, 8 * g : 8 * g + 8, :] = accs[g]

            def column(j, carry):
                flag = flag_ref[i, j].astype(f32)
                x = [
                    jnp.broadcast_to(urs[i, pl.ds(j * PACK + l, 1), :] * flag, (8, lanes))
                    for l in range(tiles)
                ]
                accs = [jnp.zeros((8, lanes), f32) for _ in range(tiles)]
                for k in range(blocks):
                    js = [
                        jac[i, j, k * 8 : (k + 1) * 8, l * lanes : (l + 1) * lanes]
                        for l in range(tiles)
                    ]
                    y = js[0] * x[0]
                    for l in range(1, tiles):
                        y = y + js[l] * x[l]
                    z = jnp.sum(y, axis=1, keepdims=True) * wt[k]
                    for l in range(tiles):
                        accs[l] = accs[l] + js[l] * z
                store_part(par, i, j, accs)
                return carry

            lax.fori_loop(0, cols, column, 0, unroll=8)
            for d in range(n_chan - 1):
                chan_copy(par, i, d).start()

        norm_v = jnp.zeros((8, lanes), f32)
        for i in range(rows):
            for g in range(cols // 2):
                r = fr[RIM + i, 8 * g + RIM * PACK : 8 * g + RIM * PACK + 8, :]
                norm_v = norm_v + r * r
        finish_chan(par)
        prod_v = norm_v
        for i in range(rows):
            for g in range(cols // 2):
                q = wide[par, WIDE + i, pl.ds(8 * g + WIDE * PACK, 8), :]
                prod_v = prod_v + urs[i, 8 * g : 8 * g + 8, :] * q
        sums[par, g_me, 0:1, :] = jnp.sum(norm_v, axis=0, keepdims=True)
        sums[par, g_me, 1:2, :] = jnp.sum(prod_v, axis=0, keepdims=True)
        for d in range(group - 1):
            sum_copy(par, d).start()
        finish_rims(par)
        for d in range(group - 1):
            sum_copy(par, d).wait_recv()
        for e in range(ext_r):
            accs = spread_back_row(par, e)
            for g in range(pairs):
                image[e, 8 * g : 8 * g + 8, :] = accs[g]
        both = sums[par, 0]
        for n in range(1, group):
            both = both + sums[par, n]
        both = jnp.sum(both, axis=1, keepdims=True)
        fresh = jnp.broadcast_to(both[0:1], (8, lanes))
        product = jnp.broadcast_to(both[1:2], (8, lanes))
        beta = jnp.where(t == 1, zero, one) * (fresh / keep[0])
        alpha = fresh / (product - beta * fresh / keep[1])
        keep[0] = fresh
        keep[1] = alpha

        for e in range(ext_r):
            for g in range(pairs):
                at = slice(8 * g, 8 * g + 8)
                r = fr[e, at, :]
                d = r + beta * fd[e, at, :]
                c = (r + image[e, at, :]) + beta * fc[e, at, :]
                fd[e, at, :] = d
                fc[e, at, :] = c
                fx[e, at, :] = fx[e, at, :] + alpha * d
                fr[e, at, :] = r - alpha * c
        finish_sends(par)
        for d in range(group - 1):
            sum_copy(par, d).wait_send()
        return carry

    lax.fori_loop(1, ITERS + 1, step, 0)

    for i in range(rows):
        accs = spread_row(fx, i)
        for g in range(cols // 2):
            urs[i, 8 * g : 8 * g + 8, :] = accs[g]
        for l in range(tiles):
            at = slice(l * lanes, (l + 1) * lanes)
            own = pl.ds(RIM * PACK + l, cols, stride=PACK)
            ctl_ref[i, :, at] = fx[RIM + i, own, :]
            res_ref[i, :, at] = fr[RIM + i, own, :]
            inc_ref[i, :, at] = urs[i, pl.ds(l, cols, stride=PACK), :]


def on_device(dims, jacobian, departures, inv_variance, channel_use, clear_flags, coefficients):
    rows, cols, chans, state = jacobian.shape
    lanes = 128
    n_along, n_across, n_chan = dims
    ext_r, ext_c = rows + 2 * RIM, cols + 2 * RIM
    field = jax.ShapeDtypeStruct((rows, cols, state), jnp.float32)
    vmem = pl.BlockSpec(memory_space=pltpu.VMEM)
    ext = pltpu.VMEM((ext_r, ext_c * PACK, lanes), jnp.float32)
    group = n_along * n_across
    return pl.pallas_call(
        functools.partial(kernel, dims),
        out_shape=(field, field, field),
        in_specs=[
            pl.BlockSpec(memory_space=pl.ANY), vmem, vmem, vmem,
            pl.BlockSpec(memory_space=pltpu.SMEM), vmem,
        ],
        out_specs=(vmem, vmem, vmem),
        scratch_shapes=[
            pltpu.VMEM((rows, cols, chans, state), jnp.float32),
            pltpu.VMEM((chans // 8, 8, lanes), jnp.float32),
            pltpu.VMEM((TAPS * TAPS, 8, lanes), jnp.float32),
            pltpu.VMEM((2, n_chan, rows * state // lanes * cols, lanes), jnp.float32),
            pltpu.VMEM((2, rows + 2 * WIDE, (cols + 2 * WIDE) * PACK, lanes), jnp.float32),
            pltpu.VMEM((2, group, 8, lanes), jnp.float32),
            pltpu.VMEM((rows, cols * PACK, lanes), jnp.float32),
            ext, ext, ext, ext, ext,
            pltpu.VMEM((2, 8, lanes), jnp.float32),
            pltpu.SemaphoreType.DMA((rows,)),
            pltpu.SemaphoreType.DMA((2, rows, n_chan)),
            pltpu.SemaphoreType.DMA((2, rows, n_chan)),
            pltpu.SemaphoreType.DMA((2, 8, max(rows, WIDE))),
            pltpu.SemaphoreType.DMA((2, 8, max(rows, WIDE))),
            pltpu.SemaphoreType.DMA((2, group)),
            pltpu.SemaphoreType.DMA((2, group)),
        ],
        compiler_params=pltpu.CompilerParams(
            collective_id=0, has_side_effects=True, vmem_limit_bytes=60 * 1024 * 1024
        ),
    )(
        jacobian, departures, inv_variance.reshape(1, chans), channel_use.reshape(1, chans),
        clear_flags, coefficients,
    )


def solution(mesh):
    dims = (mesh.shape["along"], mesh.shape["across"], mesh.shape["chan"])
    return jax.shard_map(
        functools.partial(on_device, dims),
        mesh=mesh,
        in_specs=(
            P("along", "across", "chan", None),
            P("along", "across", "chan"),
            P("chan"),
            P("chan"),
            P("along", "across"),
            P(),
        ),
        out_specs=(
            P("along", "across", None),
            P("along", "across", None),
            P("along", "across", None),
        ),
        check_vma=False,
    )
```
